128 devices in a mesh: dp: 32 (over x, z, core), mp: 4 (over y).
Axes of the slice: x: 4, y: 4, z: 4, core: 2. Of those that a mesh axis runs over, the one named last changes fastest.
Arguments:
- states: bfloat16 [64, 512, 1024], P('dp'), may hold values from -36 to 36
- retrieval: float32 [64], P('dp'), may hold values from -15 to 315
- pair_query: int32 [64], replicated, may hold values from 0 to 7, as said below
- positions: int32 [64, 64], P('dp'), may hold values from 0 to 511
- targets: int32 [64, 64], P('dp'), may hold values from 0 to 16383
- proj_weight: bfloat16 [3, 1024, 1024], P(None, None, 'mp'), may hold values from -0.1875 to 0.1875
- out_weight: bfloat16 [1024, 1024], P('mp'), may hold values from -0.1875 to 0.1875
- up_weight: bfloat16 [1024, 4096], P(None, 'mp'), may hold values from -0.1875 to 0.1875
- down_weight: bfloat16 [4096, 1024], P('mp'), may hold values from -0.09375 to 0.09375
- vocab_embed: bfloat16 [16384, 1024], P('mp'), may hold values from -3 to 3
Outputs:
- proj_grad: float32 [3, 1024, 1024], P(None, 'dp', 'mp')
- out_grad: float32 [1024, 1024], P('mp', 'dp')
- up_grad: float32 [1024, 4096], P('dp', 'mp')
- down_grad: float32 [4096, 1024], P('mp', 'dp')
- score_grad: float32 [64], P('dp')
The draws below stay inside these ranges and needn't reach their ends.
Inputs may be any that keep to these rules, and one draw needn't show every extreme that they name: `pair_query`: each query has 4 to 32 pairs and some query has exactly 32; pairs of one query lie anywhere.
All inputs are finite; a program needn't handle non-finite values.
Results may differ from the reference program's by a relative error of at most 0.019.
Values may be sent and summed in bfloat16 or wider, within the bound.
No kernel may reach another device: no remote copies, remote signals or barrier semaphores. Data moves between devices by JAX's collectives and lax.ppermute only.
A program may use at most 192 MiB of HBM per device.

```python
import math
import jax
import jax.numpy as jnp
import numpy as np
from jax import lax

D = 1024
HEAD = 64
FF = 4096
VOCAB = 16384
SEQ = 512
MASKS = 64
PAIRS_DEV = 2
PAIRS = 64
QUERIES = 8
MOST_DOCS = 32


def query_ids(key):
    queries = PAIRS // 8
    spare = MOST_DOCS - 4
    extra = jnp.zeros((queries,), jnp.int32)
    slots = (queries - 1) * spare
    if slots > 0:
        remaining = PAIRS - 4 * queries - spare
        owners = jnp.arange(slots) // spare + 1
        ranks = jax.random.permutation(jax.random.fold_in(key, 11), slots)
        taken = (ranks < remaining).astype(jnp.int32)
        extra = extra.at[owners].add(taken)
    extra = extra.at[0].add(spare)
    order = jax.random.permutation(jax.random.fold_in(key, 12), queries)
    counts = 4 + extra[order]
    bounds = jnp.cumsum(counts)
    sorted_ids = jnp.sum((jnp.arange(PAIRS)[:, None] >= bounds[None, :]).astype(jnp.int32), axis=1)
    shuffle = jax.random.permutation(jax.random.fold_in(key, 13), PAIRS)
    return sorted_ids[shuffle].astype(jnp.int32)


def draw_pair_query(key, part):
    return query_ids(key)


def draw_retrieval(key, part):
    base = jnp.clip(3.0 * jax.random.normal(jax.random.fold_in(key, 21), (PAIRS,), jnp.float32), -15.0, 15.0)
    return base


def draw_states(key, part):
    noise = jnp.clip(jax.random.normal(jax.random.fold_in(key, 41), (PAIRS, SEQ, D), jnp.float32), -6.0, 6.0)
    groups = PAIRS // PAIRS_DEV
    pairing = jax.random.permutation(jax.random.fold_in(key, 42), groups)
    pair_block = jnp.arange(PAIRS) // PAIRS_DEV
    feature_block = jnp.arange(D) // (D // groups)
    boost = jnp.where(pairing[pair_block][:, None] == feature_block[None, :], 4.0, 1.0)
    values = noise * boost[:, None, :]
    return values.astype(jnp.bfloat16)


def draw_vocab_embed(key, part):
    base = jnp.clip(0.1 * jax.random.normal(jax.random.fold_in(key, 51), (VOCAB, D), jnp.float32), -0.6, 0.6)
    return base.astype(jnp.bfloat16)


def touch_ends(entries, rng, low, high):
    longest = entries.shape.index(max(entries.shape))
    spots = []
    for shift in (0, 1):
        where = [jax.random.randint(jax.random.fold_in(rng, axis), (), 0, length) for axis, length in enumerate(entries.shape)]
        where[longest] = (where[longest] + shift) % entries.shape[longest]
        spots.append(tuple(where))
    return entries.at[spots[0]].set(low).at[spots[1]].set(high)


def block_levels(stream_key, dims, pieces, smallest, largest):
    factor_of = 1.0
    for dim, shards_of in pieces:
        heights = jax.random.uniform(jax.random.fold_in(jax.random.fold_in(stream_key, 6), dim), (shards_of,), jnp.float32, smallest / len(pieces), largest / len(pieces))
        factor_of = factor_of * jnp.repeat(jnp.exp(heights), dims[dim] // shards_of).reshape((-1,) + (1,) * (len(dims) - 1 - dim))
    return factor_of


def cumulative_ranks(number_of, slope):
    loads = [(1 << 20) // math.isqrt(standing ** slope) + 1 for standing in range(1, number_of + 1)]
    scale = 1 + sum(loads) // (1 << 30)
    return np.cumsum(np.array([max(1, weight // scale) for weight in loads]))


def ranked_ids(key, extent, number_of, lean):
    grid = cumulative_ranks(number_of, lean)
    ticket = jax.random.randint(jax.random.fold_in(key, 1), extent, 0, int(grid[number_of - 1]))
    grade = jnp.searchsorted(jnp.asarray(grid, jnp.int32), ticket, side="right")
    return jax.random.permutation(jax.random.fold_in(key, 2), number_of)[grade].astype(jnp.int32)


def gaussian(rng, dims, scale, bound, cuts=(), held_as=jnp.bfloat16):
    entries = scale * jax.random.normal(rng, dims, jnp.float32)
    if cuts:
        entries = entries * block_levels(rng, dims, cuts, -0.22, 0.18)
    return jnp.clip(entries, -bound, bound).astype(held_as)


def setup_inputs(seed: int = 0) -> dict:
    seeds = jax.random.split(jax.random.key(seed), 11)
    states = draw_states(jax.random.fold_in(seeds[10], 71), 0)
    retrieval = draw_retrieval(jax.random.fold_in(seeds[10], 71), 0)
    pair_query = draw_pair_query(jax.random.fold_in(seeds[10], 71), 0)
    positions = touch_ends(jax.random.randint(seeds[3], (PAIRS, MASKS), 0, SEQ), jax.random.fold_in(seeds[3], 1), 0, SEQ - 1).astype(jnp.int32)
    targets = touch_ends(ranked_ids(seeds[4], (PAIRS, MASKS), VOCAB, 2), jax.random.fold_in(seeds[4], 3), 0, VOCAB - 1).astype(jnp.int32)
    proj_weight = gaussian(seeds[5], (3, D, D), D ** -0.5, 0.1875, ((2, 4),))
    out_weight = gaussian(seeds[6], (D, D), D ** -0.5, 0.1875, ((0, 4),))
    up_weight = gaussian(seeds[7], (D, FF), D ** -0.5, 0.1875, ((1, 4),))
    down_weight = gaussian(seeds[8], (FF, D), FF ** -0.5, 0.09375, ((0, 4),))
    vocab_embed = draw_vocab_embed(jax.random.fold_in(seeds[10], 71), 0)
    return dict(states=states, retrieval=retrieval, pair_query=pair_query, positions=positions, targets=targets, proj_weight=proj_weight, out_weight=out_weight, up_weight=up_weight, down_weight=down_weight, vocab_embed=vocab_embed)


def round_trip(value):
    return lax.optimization_barrier(value.astype(jnp.bfloat16)).astype(jnp.float32)

def matmul(left, right):
    return jnp.dot(left, right, preferred_element_type=jnp.float32)

def matmul_tn(left, right):
    return lax.dot_general(left, right, (((0,), (0,)), ((), ())), preferred_element_type=jnp.float32)

def matmul_nt(left, right):
    return lax.dot_general(left, right, (((1,), (1,)), ((), ())), preferred_element_type=jnp.float32)

def layer_norm(value):
    centre = lax.optimization_barrier(jnp.mean(value, axis=-1, keepdims=True))
    centred = value - centre
    spread = lax.optimization_barrier(jnp.mean(centred * centred, axis=-1, keepdims=True))
    return centred * lax.rsqrt(spread + 1e-05)

def norm_back(value, cotangent):
    return jax.vjp(layer_norm, value)[1](cotangent)[0]

def gelu_tanh(value):
    return jax.nn.gelu(value, approximate=True)

def gelu_back(value, cotangent):
    return jax.vjp(gelu_tanh, value)[1](cotangent)[0]

def attention(projected):
    seq_len = projected.shape[1]
    head_count = projected.shape[2] // HEAD
    parts = projected.astype(jnp.float32).reshape(3, seq_len, head_count, HEAD)
    scores = jnp.einsum('qhd,khd->hqk', parts[0], parts[1]) * HEAD ** (-0.5)
    top_value = lax.optimization_barrier(jnp.max(scores, axis=-1, keepdims=True))
    weights = jnp.exp(scores - top_value)
    probs = round_trip(weights / lax.optimization_barrier(jnp.sum(weights, axis=-1, keepdims=True)))
    context = jnp.einsum('hqk,khd->qhd', probs, parts[2])
    return context.reshape(seq_len, head_count * HEAD)

def attention_back(projected, cotangent):
    return jax.vjp(attention, projected)[1](cotangent.astype(jnp.float32))[0]

def forward(states, proj_weight, out_weight, up_weight, down_weight):
    projected = jnp.stack([matmul(states, proj_weight[part_num]) for part_num in range(3)]).astype(jnp.bfloat16)
    context = attention(projected).astype(jnp.bfloat16)
    pre_one = states.astype(jnp.float32) + matmul(context, out_weight)
    first_norm = layer_norm(pre_one).astype(jnp.bfloat16)
    inner_act = matmul(first_norm, up_weight)
    activated = gelu_tanh(inner_act).astype(jnp.bfloat16)
    pre_two = first_norm.astype(jnp.float32) + matmul(activated, down_weight)
    final_norm = layer_norm(pre_two).astype(jnp.bfloat16)
    return (projected, context, pre_one, first_norm, inner_act, activated, pre_two, final_norm)

def vocab_terms(picked, targets, vocab_embed):
    logits = matmul_nt(picked, vocab_embed)
    top_value = lax.optimization_barrier(jnp.max(logits, axis=1))
    exp_terms = jnp.exp(logits - top_value[:, None])
    denominator = lax.optimization_barrier(jnp.sum(exp_terms, axis=1))
    target_logit = jnp.take_along_axis(logits, targets[:, None], axis=1)[:, 0]
    log_prob = target_logit - top_value - jnp.log(denominator)
    return (log_prob, exp_terms / denominator[:, None])

def masked_max(values, member):
    return lax.optimization_barrier(jnp.max(jnp.where(member, values[:, None], -1e+30), axis=0))

def masked_sum(values, member, top_value):
    shifted = jnp.where(member, values[:, None] - top_value[None, :], -1e+30)
    return lax.optimization_barrier(jnp.sum(jnp.where(member, jnp.exp(shifted), 0.0), axis=0))

def query_lse(values, member):
    top_value = masked_max(values, member)
    return top_value + jnp.log(masked_sum(values, member, top_value))

def per_pair(per_query, member):
    return lax.optimization_barrier(jnp.sum(jnp.where(member, per_query[None, :], 0.0), axis=1))

def reference(states, retrieval, pair_query, positions, targets, proj_weight, out_weight, up_weight, down_weight, vocab_embed):

    def likelihood(item):
        pair_states, pair_pos, pair_tgt = item
        final_norm = forward(pair_states, proj_weight, out_weight, up_weight, down_weight)[7]
        picked = jnp.take(final_norm, pair_pos, axis=0)
        log_prob = vocab_terms(picked, pair_tgt, vocab_embed)[0]
        return jnp.sum(log_prob) / MASKS
    doc_ll = lax.map(likelihood, (states, positions, targets))
    member = pair_query[:, None] == jnp.arange(QUERIES)[None, :]
    post_values = retrieval + doc_ll
    posterior = jnp.exp(post_values - per_pair(query_lse(post_values, member), member))
    prior = jnp.exp(retrieval - per_pair(query_lse(retrieval, member), member))
    score_grad = prior - posterior

    def accumulate(carry, item):
        pair_states, pair_pos, pair_tgt, weight = item
        projected, context, pre_one, first_norm, inner_act, activated, pre_two, final_norm = forward(pair_states, proj_weight, out_weight, up_weight, down_weight)
        picked = jnp.take(final_norm, pair_pos, axis=0)
        probs = vocab_terms(picked, pair_tgt, vocab_embed)[1]
        target_hot = (pair_tgt[:, None] == jnp.arange(VOCAB)[None, :]).astype(jnp.float32)
        dlogit = (weight / MASKS * (probs - target_hot)).astype(jnp.bfloat16)
        dpicked = matmul(dlogit, vocab_embed)
        dfinal = jnp.zeros((SEQ, D), jnp.float32).at[pair_pos].add(dpicked)
        dpre_two = norm_back(pre_two, dfinal).astype(jnp.bfloat16)
        down_term = matmul_tn(activated, dpre_two)
        dinner = gelu_back(inner_act, matmul_nt(dpre_two, down_weight)).astype(jnp.bfloat16)
        up_term = matmul_tn(first_norm, dinner)
        dfirst = dpre_two.astype(jnp.float32) + matmul_nt(dinner, up_weight)
        dpre_one = norm_back(pre_one, dfirst).astype(jnp.bfloat16)
        out_term = matmul_tn(context, dpre_one)
        dcontext = matmul_nt(dpre_one, out_weight).astype(jnp.bfloat16)
        dprojected = attention_back(projected, dcontext)
        proj_term = jnp.stack([matmul_tn(pair_states, dprojected[part_num]) for part_num in range(3)])
        return ((carry[0] + proj_term, carry[1] + out_term, carry[2] + up_term, carry[3] + down_term), None)
    zeros = (jnp.zeros((3, D, D), jnp.float32), jnp.zeros((D, D), jnp.float32), jnp.zeros((D, FF), jnp.float32), jnp.zeros((FF, D), jnp.float32))
    grads = lax.scan(accumulate, zeros, (states, positions, targets, posterior))[0]
    return (grads[0], grads[1], grads[2], grads[3], score_grad)
```

```python
import jax
import jax.numpy as jnp
from jax import lax
from jax.sharding import PartitionSpec as P

HEAD = 64
NX, NZ, NC = 4, 4, 2


def dot(left, right, dims):
    return lax.dot_general(left, right, (dims, ((), ())), preferred_element_type=jnp.float32)


def mm(left, right):
    return dot(left, right, ((1,), (0,)))


def mm_tn(left, right):
    return dot(left, right, ((0,), (0,)))


def mm_nt(left, right):
    return dot(left, right, ((1,), (1,)))


def ring(size, shift):
    return [(i, (i + shift) % size) for i in range(size)]


def dp_index(x, z, c):
    return (x * NZ + z) * NC + c


def x_ring(shift):
    return [
        (dp_index(x, z, c), dp_index((x + shift) % NX, z, c))
        for x in range(NX) for z in range(NZ) for c in range(NC)
    ]


def z_ring(shift):
    return [
        (dp_index(x, z, c), dp_index(x, (z + shift) % NZ, c))
        for x in range(NX) for z in range(NZ) for c in range(NC)
    ]


CORE_SWAP = [
    (dp_index(x, z, c), dp_index(x, z, 1 - c)) for x in range(NX) for z in range(NZ) for c in range(NC)
]


def mp_all(value):
    size = lax.axis_size("mp")
    return [value] + [lax.ppermute(value, "mp", ring(size, d)) for d in range(1, size)]


def mp_sum(partial):
    return sum(v.astype(jnp.float32) for v in mp_all(partial.astype(jnp.bfloat16)))


def norm_parts(value):
    centre = jnp.mean(value, axis=-1, keepdims=True)
    centred = value - centre
    scale = lax.rsqrt(jnp.mean(centred * centred, axis=-1, keepdims=True) + 1e-05)
    return centred * scale, scale


def norm_back(hat, scale, cot):
    first = jnp.mean(cot, axis=-1, keepdims=True)
    second = jnp.mean(cot * hat, axis=-1, keepdims=True)
    return scale * (cot - first - hat * second)


def gelu(value):
    return jax.nn.gelu(value, approximate=True)


def gelu_slope(value, cot):
    return jax.vjp(gelu, value)[1](cot)[0]


def phase(blocks, own, size, ring_of):
    total = lax.dynamic_index_in_dim(blocks, own, 0, keepdims=False)
    for d in range(1, size):
        send = lax.dynamic_index_in_dim(blocks, lax.rem(own + d, size), 0, keepdims=False)
        total += lax.ppermute(send.astype(jnp.bfloat16), "dp", ring_of(d)).astype(jnp.float32)
    return total


def reduce_rows(grad, index):
    rows, cols = grad.shape
    own_x, own_z, own_c = index // (NZ * NC), index // NC % NZ, index % NC
    blocks = grad.reshape(NX, NZ, NC, rows // (NX * NZ * NC), cols)
    keep = lax.dynamic_index_in_dim(blocks, own_c, 2, keepdims=False)
    send = lax.dynamic_index_in_dim(blocks, 1 - own_c, 2, keepdims=False)
    blocks = keep + lax.ppermute(send.astype(jnp.bfloat16), "dp", CORE_SWAP).astype(jnp.float32)
    half = cols // 2
    one = phase(blocks[..., :half], own_x, NX, x_ring)
    two = phase(jnp.swapaxes(blocks[..., half:], 0, 1), own_z, NZ, z_ring)
    one = phase(one, own_z, NZ, z_ring)
    two = phase(two, own_x, NX, x_ring)
    return jnp.concatenate([one, two], axis=-1)


def gather_dp(values):
    core = lax.axis_index("dp") % NC
    swapped = lax.ppermute(values, "dp", CORE_SWAP)
    both = jnp.stack([jnp.where(core == 0, values, swapped), jnp.where(core == 0, swapped, values)])
    own_z = lax.axis_index("dp") // NC % NZ
    own_x = lax.axis_index("dp") // (NC * NZ)

    def collect(block, own, size, ring_of):
        got = jnp.stack([block] + [lax.ppermute(block, "dp", ring_of(d)) for d in range(1, size)])
        order = lax.rem(own - jnp.arange(size) + size, size)
        hot = order[:, None] == jnp.arange(size)[None, :]
        return jnp.sum(jnp.where(hot.reshape(size, size, *([1] * block.ndim)), got[:, None], 0.0), axis=0)

    rows = collect(both, own_z, NZ, z_ring)
    return collect(rows, own_x, NX, x_ring).reshape(NX * NZ * NC, -1)


def local(
    states, retrieval, pair_query, positions, targets,
    proj_weight, out_weight, up_weight, down_weight, vocab_embed,
):
    bf = jnp.bfloat16
    pairs, seq, width = states.shape
    masks = positions.shape[1]
    rows = pairs * masks
    cols = proj_weight.shape[2]
    heads = cols // HEAD
    index = lax.axis_index("dp")
    flat = states.reshape(pairs * seq, width)

    place = (positions[:, :, None] == jnp.arange(seq)[None, None, :]).astype(bf)
    picked = jnp.concatenate([mm(place[p], states[p]) for p in range(pairs)]).astype(bf)
    query = mm(picked, proj_weight[0]).astype(bf)
    key = mm(flat, proj_weight[1]).astype(bf)
    val = mm(flat, proj_weight[2]).astype(bf)
    head_of = jnp.arange(cols) // HEAD
    head_mask = jnp.arange(heads)[:, None, None] == head_of[None, None, :]

    def stack_heads(block):
        return jnp.where(head_mask, block[None], 0).astype(bf).reshape(heads * masks, cols)

    def join_heads(block):
        return jnp.sum(jnp.where(head_mask, block.reshape(heads, masks, cols), 0.0), axis=0)

    soft, probs, context = [], [], []
    for p in range(pairs):
        scores = mm_nt(stack_heads(query[p * masks:(p + 1) * masks]), key[p * seq:(p + 1) * seq])
        scores = scores * HEAD ** (-0.5)
        weights = jnp.exp(scores - jnp.max(scores, axis=-1, keepdims=True))
        weights = weights / jnp.sum(weights, axis=-1, keepdims=True)
        soft.append(weights)
        probs.append(weights.astype(bf))
        context.append(join_heads(mm(probs[p], val[p * seq:(p + 1) * seq])))
    context = jnp.concatenate(context).astype(bf)
    pre_one = picked.astype(jnp.float32) + mp_sum(mm(context, out_weight))
    hat_one, scale_one = norm_parts(pre_one)
    first = hat_one.astype(bf)
    inner = mm(first, up_weight)
    activated = gelu(inner).astype(bf)
    pre_two = first.astype(jnp.float32) + mp_sum(mm(activated, down_weight))
    hat_two, scale_two = norm_parts(pre_two)
    final = hat_two.astype(bf)

    logits = mm_nt(final, vocab_embed)
    vocab_local = vocab_embed.shape[0]
    local_target = targets.reshape(-1) - lax.axis_index("mp") * vocab_local
    hot = local_target[:, None] == jnp.arange(vocab_local)[None, :]
    own_top = jnp.max(logits, axis=1)
    rest = jnp.where(hot, 0.0, jnp.exp(logits - own_top[:, None]))
    own_rest = jnp.sum(rest, axis=1)
    own_logit = jnp.sum(jnp.where(hot, logits, 0.0), axis=1)
    has = (local_target >= 0) & (local_target < vocab_local)
    target_rows = jnp.where(has[:, None], vocab_embed[jnp.clip(local_target, 0, vocab_local - 1)], 0)
    stats = mp_all(jnp.stack([own_top, own_rest, own_logit]))
    part = mm(rest.astype(bf), vocab_embed)
    target_logit = sum(s[2] for s in stats)
    top = stats[0][0]
    for s in stats[1:]:
        top = jnp.maximum(top, s[0])
    rest_sum = sum(s[1] * jnp.exp(s[0] - top) for s in stats)
    denominator = rest_sum + jnp.exp(target_logit - top)
    log_prob = target_logit - top - jnp.log(denominator)
    doc_ll = jnp.sum(log_prob.reshape(pairs, masks), axis=1) / masks
    dpart = (jnp.exp(own_top - top) / denominator)[:, None] * part - (
        rest_sum / denominator
    )[:, None] * target_rows.astype(jnp.float32)
    dfinal = mp_sum(dpart)

    gathered = gather_dp(jnp.concatenate([retrieval, retrieval + doc_ll]))
    all_prior = gathered[:, :pairs].reshape(-1)
    all_post = gathered[:, pairs:].reshape(-1)
    own_query = lax.dynamic_slice_in_dim(pair_query, index * pairs, pairs, 0)
    same = own_query[:, None] == pair_query[None, :]

    def share(values, own):
        top_value = jnp.max(jnp.where(same, values[None, :], -1e30), axis=1)
        total = jnp.sum(jnp.where(same, jnp.exp(jnp.where(same, values[None, :] - top_value[:, None], 0.0)), 0.0), axis=1)
        return jnp.exp(own - (top_value + jnp.log(total)))

    posterior = share(all_post, retrieval + doc_ll)
    prior = share(all_prior, retrieval)
    score_grad = prior - posterior
    weight = (posterior / masks)[:, None]

    def scaled(block):
        per = block.shape[0] // pairs
        return (block.reshape(pairs, per, -1) * weight[:, :, None]).reshape(block.shape).astype(bf)

    dpre_two = norm_back(hat_two, scale_two, dfinal).astype(bf)
    dinner = gelu_slope(inner, mm_nt(dpre_two, down_weight)).astype(bf)
    dfirst = dpre_two.astype(jnp.float32) + mp_sum(mm_nt(dinner, up_weight))
    down_term = mm_tn(scaled(dpre_two), activated)
    up_term = mm_tn(first, scaled(dinner))
    dpre_one = norm_back(hat_one, scale_one, dfirst).astype(bf)
    out_term = mm_tn(scaled(dpre_one), context)
    dcontext = mm_nt(dpre_one, out_weight).astype(bf)
    dquery, dkey, dval = [], [], []
    for p in range(pairs):
        stacked = stack_heads(dcontext[p * masks:(p + 1) * masks])
        k_p, v_p = key[p * seq:(p + 1) * seq], val[p * seq:(p + 1) * seq]
        dval.append(mm_tn(probs[p], stacked))
        dprobs = mm_nt(stacked, v_p).astype(bf).astype(jnp.float32)
        dscores = soft[p] * (dprobs - jnp.sum(dprobs * soft[p], axis=-1, keepdims=True))
        dscores = (dscores * HEAD ** (-0.5)).astype(bf)
        dquery.append(join_heads(mm(dscores, k_p)))
        dkey.append(mm_tn(dscores, stack_heads(query[p * masks:(p + 1) * masks])))
    dquery, dkey, dval = [scaled(jnp.concatenate(v)) for v in (dquery, dkey, dval)]
    grads = jnp.concatenate(
        [down_term, up_term, out_term, mm_tn(picked, dquery), mm_tn(flat, dkey), mm_tn(flat, dval)], axis=1
    )
    total = reduce_rows(grads, index)
    hidden = up_weight.shape[1]
    down_grad = total[:, :hidden].T
    up_grad = total[:, hidden:2 * hidden]
    out_grad = total[:, 2 * hidden:2 * hidden + cols].T
    proj_grad = jnp.stack(
        [total[:, 2 * hidden + (i + 1) * cols:2 * hidden + (i + 2) * cols] for i in range(3)]
    )
    return proj_grad, out_grad, up_grad, down_grad, score_grad


def solution(mesh):
    return jax.shard_map(
        local,
        mesh=mesh,
        in_specs=(
            P("dp", None, None),
            P("dp"),
            P(),
            P("dp", None),
            P("dp", None),
            P(None, None, "mp"),
            P("mp", None),
            P(None, "mp"),
            P("mp", None),
            P("mp", None),
        ),
        out_specs=(P(None, "dp", "mp"), P("mp", "dp"), P("dp", "mp"), P("mp", "dp"), P("dp")),
        check_vma=False,
    )
```

```python
import functools

import jax
import jax.numpy as jnp
from jax import lax
from jax.experimental import pallas as pl
from jax.experimental.pallas import tpu as pltpu
from jax.sharding import PartitionSpec as P

HEAD = 64
NX, NZ, NC = 4, 4, 2
NP = NX * NZ
ROW = 32
BF = jnp.bfloat16
F32 = jnp.float32


def dot(left, right, dims):
    return lax.dot_general(left, right, (dims, ((), ())), preferred_element_type=F32)


def mm(left, right):
    return dot(left, right, ((1,), (0,)))


def mm_tn(left, right):
    return dot(left, right, ((0,), (0,)))


def mm_nt(left, right):
    return dot(left, right, ((1,), (1,)))


def iota(shape, dim):
    return lax.broadcasted_iota(jnp.int32, shape, dim)


def norm_parts(value):
    centre = jnp.mean(value, axis=-1, keepdims=True)
    centred = value - centre
    scale = lax.rsqrt(jnp.mean(centred * centred, axis=-1, keepdims=True) + 1e-05)
    return centred * scale, scale


def norm_back(hat, scale, cot):
    first = jnp.mean(cot, axis=-1, keepdims=True)
    second = jnp.mean(cot * hat, axis=-1, keepdims=True)
    return scale * (cot - first - hat * second)


def gelu_parts(value):
    root = 0.7978845608028654
    return jnp.tanh(root * (value + 0.044715 * value * value * value))


def gelu_slope(value):
    root = 0.7978845608028654
    bend = gelu_parts(value)
    return 0.5 * (1.0 + bend) + 0.5 * value * (1.0 - bend * bend) * root * (1.0 + 3.0 * 0.044715 * value * value)


def to_column(row):
    size = row.shape[1]
    eye = iota((size, size), 0) == iota((size, size), 1)
    return jnp.sum(jnp.where(eye, row, jnp.zeros_like(row)), axis=1, keepdims=True)


def to_row(column):
    size = column.shape[0]
    eye = iota((size, size), 0) == iota((size, size), 1)
    return jnp.sum(jnp.where(eye, column, jnp.zeros_like(column)), axis=0, keepdims=True)


def head_mask(rows, cols):
    return iota((rows, cols), 0) // (rows * HEAD // cols) == iota((rows, cols), 1) // HEAD


def stack_heads(block):
    masks, cols = block.shape
    heads = cols // HEAD
    tiled = jnp.concatenate([block] * heads, axis=0)
    return jnp.where(head_mask(heads * masks, cols), tiled.astype(F32), 0.0).astype(block.dtype)


def join_heads(block, masks):
    cols = block.shape[1]
    kept = jnp.where(head_mask(block.shape[0], cols), block, 0.0)
    return sum(kept[h * masks:(h + 1) * masks] for h in range(cols // HEAD))


def selector(width, core):
    half = width // 2
    col = iota((width, half), 1)
    return (iota((width, half), 0) == col // ROW * (2 * ROW) + core * ROW + col % ROW).astype(F32).astype(BF)


def total(refs):
    return sum(r[...].astype(F32) for r in refs)


def k_attend(core, pos, x, wp, wo, o_xp, o_q, o_k, o_v, o_soft, o_ctx, o_part):
    pairs, masks = pos.shape
    seq = x.shape[0] // pairs
    for p in range(pairs):
        rows, cols = pl.ds(p * masks, masks), pl.ds(p * seq, seq)
        x_p = x[cols, :]
        place = (iota((seq, masks), 0) == pos[p:p + 1, :]).astype(F32).astype(BF)
        picked = mm_tn(place, x_p).astype(BF)
        o_xp[rows, :] = picked
        query = mm(picked, wp[0]).astype(BF)
        key = mm(x_p, wp[1]).astype(BF)
        val = mm(x_p, wp[2]).astype(BF)
        o_q[rows, :] = query
        o_k[cols, :] = key
        o_v[cols, :] = val
        scores = mm_nt(stack_heads(query), key) * HEAD ** (-0.5)
        weights = jnp.exp(scores - jnp.max(scores, axis=-1, keepdims=True))
        soft = weights / jnp.sum(weights, axis=-1, keepdims=True)
        o_soft[pl.ds(p * soft.shape[0], soft.shape[0]), :] = soft
        o_ctx[rows, :] = join_heads(mm(soft.astype(BF), val), masks).astype(BF)
    o_part[...] = mm(o_ctx[...], wo[...]).astype(BF)


def k_split(core, x, xp, ctx, o_mine, o_other, o_send):
    width = x.shape[1]
    mine, other = selector(width, core[0]), selector(width, 1 - core[0])
    o_mine[...] = mm(x[...], mine).astype(BF)
    o_other[...] = mm(x[...], other).astype(BF)
    o_send[:, :width // 2] = mm(xp[...], other).astype(BF)
    o_send[:, width // 2:] = ctx[...]


def k_feed(core, xp, p0, p1, p2, p3, up, down, o_hat, o_scale, o_inner, o_part, o_send):
    pre_one = xp[...].astype(F32) + total((p0, p1, p2, p3))
    hat, scale = norm_parts(pre_one)
    o_hat[...] = hat
    o_scale[...] = jnp.broadcast_to(scale, o_scale.shape)
    first = hat.astype(BF)
    inner = mm(first, up[...])
    o_inner[...] = inner
    act = (0.5 * inner * (1.0 + gelu_parts(inner))).astype(BF)
    o_part[...] = mm(act, down[...]).astype(BF)
    hidden = inner.shape[1]
    o_send[:, :hidden] = act
    o_send[:, hidden:] = mm(first, selector(first.shape[1], 1 - core[0])).astype(BF)


CHUNK = 1024


def k_logits(base, hat, p0, p1, p2, p3, tgt, emb, o_hat, o_scale, o_exp, o_stat, logits):
    pre_two = hat[...].astype(BF).astype(F32) + total((p0, p1, p2, p3))
    hat_two, scale = norm_parts(pre_two)
    o_hat[...] = hat_two
    o_scale[...] = jnp.broadcast_to(scale, o_scale.shape)
    final = hat_two.astype(BF)
    rows = final.shape[0]
    target = jnp.concatenate([to_column(tgt[p:p + 1, :]) for p in range(tgt.shape[0])], axis=0) - base[0]
    top = jnp.full((rows, 1), -jnp.inf, F32)
    own = jnp.zeros((rows, 1), F32)
    steps = emb.shape[0] // CHUNK
    for j in range(steps):
        part = mm_nt(final, emb[j * CHUNK:(j + 1) * CHUNK, :])
        logits[:, j * CHUNK:(j + 1) * CHUNK] = part
        hot = iota((rows, CHUNK), 1) + j * CHUNK == target
        top = jnp.maximum(top, jnp.max(part, axis=1, keepdims=True))
        own += jnp.sum(jnp.where(hot, part, 0.0), axis=1, keepdims=True)
    rest = jnp.zeros((rows, 1), F32)
    for j in range(steps):
        hot = iota((rows, CHUNK), 1) + j * CHUNK == target
        value = jnp.where(hot, 0.0, jnp.exp(logits[:, j * CHUNK:(j + 1) * CHUNK] - top))
        o_exp[:, j * CHUNK:(j + 1) * CHUNK] = value.astype(BF)
        rest += jnp.sum(value, axis=1, keepdims=True)
    line = iota(o_stat.shape, 0)
    o_stat[...] = jnp.where(line == 0, to_row(top), jnp.where(line == 1, to_row(rest), jnp.where(line == 2, to_row(own), 0.0)))


def k_vocab(base, exps, tgt, emb, o_sum, o_row):
    rows = exps.shape[0]
    target = jnp.concatenate([to_column(tgt[p:p + 1, :]) for p in range(tgt.shape[0])], axis=0) - base[0]
    acc = jnp.zeros((2 * rows, emb.shape[1]), F32)
    for j in range(emb.shape[0] // CHUNK):
        hot = (iota((rows, CHUNK), 1) + j * CHUNK == target).astype(F32).astype(BF)
        left = jnp.concatenate([exps[:, j * CHUNK:(j + 1) * CHUNK], hot], axis=0)
        acc += mm(left, emb[j * CHUNK:(j + 1) * CHUNK, :])
    o_sum[...] = acc[:rows]
    o_row[...] = acc[rows:].astype(BF)


def k_join(index, retrieval, s0, s1, s2, s3, sums, erow, o_part, o_vals):
    stats = (s0, s1, s2, s3)
    top = s0[0:1, :]
    for s in stats[1:]:
        top = jnp.maximum(top, s[0:1, :])
    rest = sum(s[1:2, :] * jnp.exp(s[0:1, :] - top) for s in stats)
    goal = sum(s[2:3, :] for s in stats)
    denominator = rest + jnp.exp(goal - top)
    log_prob = goal - top - jnp.log(denominator)
    own = jnp.exp(s0[0:1, :] - top) / denominator
    o_part[...] = (to_column(own) * sums[...] - to_column(rest / denominator) * erow[...].astype(F32)).astype(BF)
    pairs = retrieval.shape[0]
    rows = log_prob.shape[1]
    masks = rows // pairs
    lane, line = iota((8, 128), 1), iota((8, 128), 0)
    vals = jnp.zeros((8, 128), F32)
    part_of = iota((1, rows), 1) // masks
    for p in range(pairs):
        doc = jnp.sum(jnp.where(part_of == p, log_prob, 0.0), axis=1, keepdims=True) / masks
        here = lane == index[0] * pairs + p
        vals += jnp.where(here & (line == 0), retrieval[p], 0.0)
        vals += jnp.where(here & (line == 1), retrieval[p] + doc, 0.0)
    o_vals[...] = jnp.broadcast_to(vals[None], o_vals.shape)


def k_back(core, index, vals, pq, p0, p1, p2, p3, hat, scale, inner, up, down, o_dpre, o_part, o_half, o_send, o_w, o_score, pairs):
    summed = jnp.sum(vals[...], axis=0)
    count = pq.shape[1]
    lane = iota((1, count), 1)
    priors, posts = summed[0:1, :count], summed[1:2, :count]
    spot = iota((8, 128), 1)
    line = iota((8, 128), 0)
    score = jnp.zeros((8, 128), F32)
    weights = jnp.zeros((8, 128), F32)
    per = []
    rows = hat.shape[0]
    masks = rows // pairs
    for p in range(pairs):
        here = lane == index[0] * pairs + p
        query = jnp.sum(jnp.where(here, pq[...], 0), axis=1, keepdims=True)
        same = pq[...] == query

        def share(values):
            top = jnp.max(jnp.where(same, values, -1e30), axis=1, keepdims=True)
            terms = jnp.where(same, jnp.exp(jnp.where(same, values - top, 0.0)), 0.0)
            own = jnp.sum(jnp.where(here, values, 0.0), axis=1, keepdims=True)
            return jnp.exp(own - (top + jnp.log(jnp.sum(terms, axis=1, keepdims=True))))

        posterior = share(posts)
        score += jnp.where((spot == p) & (line == 0), share(priors) - posterior, 0.0)
        weights += jnp.where(line == p, posterior / masks, 0.0)
        per.append(jnp.broadcast_to(posterior / masks, (masks, 1)))
    o_w[...] = weights
    o_score[...] = score
    weight = jnp.concatenate(per, axis=0)
    dpre = norm_back(hat[...], scale[:, 0:1], total((p0, p1, p2, p3))).astype(BF)
    o_dpre[...] = dpre
    dinner = (gelu_slope(inner[...]) * mm_nt(dpre, down[...])).astype(BF)
    o_part[...] = mm_nt(dinner, up[...]).astype(BF)
    width = dpre.shape[1]
    scaled = (dpre.astype(F32) * weight).astype(BF)
    o_half[:, :width // 2] = mm(scaled, selector(width, core[0])).astype(BF)
    dinner = (dinner.astype(F32) * weight).astype(BF)
    o_half[:, width // 2:] = dinner
    o_send[:, :width // 2] = mm(scaled, selector(width, 1 - core[0])).astype(BF)
    o_send[:, width // 2:] = dinner


def k_early(core, hat, own_f, got_f, own_b, got_b, out):
    rows, width = hat.shape
    half = width // 2
    hidden = own_f.shape[1] - half
    first = mm(hat[...].astype(BF), selector(width, core[0])).astype(BF)
    left = jnp.concatenate([own_b[:, :half], got_b[:, :half]], axis=0)
    right = jnp.concatenate([own_f[:, :hidden], got_f[:, :hidden]], axis=0)
    down = mm_tn(left, right).astype(BF)
    left = jnp.concatenate([first, got_f[:, hidden:]], axis=0)
    right = jnp.concatenate([own_b[:, half:], got_b[:, half:]], axis=0)
    up = mm_tn(left, right).astype(BF)
    for i in range(out.shape[0]):
        out[i, :, :hidden] = down[i * ROW:(i + 1) * ROW]
        out[i, :, hidden:] = up[i * ROW:(i + 1) * ROW]


def k_attend_back(core, w, p0, p1, p2, p3, dpre_two, hat, scale, wo, q, k, v, soft, o_kv, o_mine, o_send):
    rows, width = hat.shape
    cols = q.shape[1]
    pairs = k.shape[0] // soft.shape[1]
    masks = rows // pairs
    seq = soft.shape[1]
    dfirst = dpre_two[...].astype(F32) + total((p0, p1, p2, p3))
    dpre = norm_back(hat[...], scale[:, 0:1], dfirst).astype(BF)
    dctx = mm_nt(dpre, wo[...]).astype(BF)
    weight = jnp.concatenate([jnp.broadcast_to(w[p:p + 1, 0:1], (masks, 1)) for p in range(pairs)], axis=0)
    scaled = (dpre.astype(F32) * weight).astype(BF)
    half = width // 2
    o_mine[:, :half] = mm(scaled, selector(width, core[0])).astype(BF)
    o_send[:, :half] = mm(scaled, selector(width, 1 - core[0])).astype(BF)
    size = soft.shape[0] // pairs
    for p in range(pairs):
        own = w[p:p + 1, 0:1]
        lines = pl.ds(p * masks, masks)
        stacked = stack_heads(dctx[p * masks:(p + 1) * masks])
        prob = soft[p * size:(p + 1) * size, :]
        o_kv[pl.ds(p * seq, seq), cols:] = (mm_tn(prob.astype(BF), stacked) * own).astype(BF)
        dprob = mm_nt(stacked, v[p * seq:(p + 1) * seq, :]).astype(BF).astype(F32)
        dscore = prob * (dprob - jnp.sum(dprob * prob, axis=-1, keepdims=True))
        dscore = (dscore * HEAD ** (-0.5)).astype(BF)
        dquery = (join_heads(mm(dscore, k[p * seq:(p + 1) * seq, :]), masks) * own).astype(BF)
        o_mine[lines, half:] = dquery
        o_send[lines, half:] = dquery
        o_kv[pl.ds(p * seq, seq), :cols] = (mm_tn(dscore, stack_heads(q[lines, :])) * own).astype(BF)


def k_late(core, x_mine, x_got, xp, ctx, fwd, kv, kv_got, own, got, out):
    width = xp.shape[1]
    half = width // 2
    cols = ctx.shape[1]
    xp_half = mm(xp[...], selector(width, core[0])).astype(BF)
    d_out = mm_tn(
        jnp.concatenate([own[:, :half], got[:, :half]], axis=0), jnp.concatenate([ctx[...], fwd[:, half:]], axis=0)
    ).astype(BF)
    d_q = mm_tn(
        jnp.concatenate([xp_half, fwd[:, :half]], axis=0), jnp.concatenate([own[:, half:], got[:, half:]], axis=0)
    ).astype(BF)
    d_kv = (mm_tn(x_mine[...], kv[...]) + mm_tn(x_got[...], kv_got[...])).astype(BF)
    for i in range(out.shape[0]):
        lines = slice(i * ROW, (i + 1) * ROW)
        out[i, :, :cols] = d_out[lines]
        out[i, :, cols:2 * cols] = d_q[lines]
        out[i, :, 2 * cols:] = d_kv[lines]


def k_sum_early(got, o_down, o_up):
    hidden = o_up.shape[1]
    value = jnp.sum(got[...].astype(F32), axis=0)
    o_down[...] = value[:, :hidden].T
    o_up[...] = value[:, hidden:]


def k_sum_late(got, o_out, o_proj):
    cols = o_out.shape[0]
    value = jnp.sum(got[...].astype(F32), axis=0)
    o_out[...] = value[:, :cols].T
    for i in range(o_proj.shape[0]):
        o_proj[i] = value[:, (i + 1) * cols:(i + 2) * cols]


def call(body, outs, args, scalars=0, scratch=(), mib=24, flops=0, name=None):
    vmem = pl.BlockSpec(memory_space=pltpu.VMEM)
    smem = pl.BlockSpec(memory_space=pltpu.SMEM)
    moved = sum(a.size * a.dtype.itemsize for a in args)
    return pl.pallas_call(
        body,
        out_shape=[jax.ShapeDtypeStruct(s, d) for s, d in outs],
        in_specs=[smem] * scalars + [vmem] * (len(args) - scalars),
        out_specs=[vmem] * len(outs),
        scratch_shapes=list(scratch),
        compiler_params=pltpu.CompilerParams(vmem_limit_bytes=mib << 20),
        cost_estimate=pl.CostEstimate(flops=flops, bytes_accessed=moved, transcendentals=0),
        name=name,
    )(*args)


def ring(size, shift):
    return [(i, (i + shift) % size) for i in range(size)]


def dp_index(x, z, c):
    return (x * NZ + z) * NC + c


CORE_SWAP = [
    (dp_index(x, z, c), dp_index(x, z, 1 - c)) for x in range(NX) for z in range(NZ) for c in range(NC)
]
PLANES = [[dp_index(x, z, c) for x in range(NX) for z in range(NZ)] for c in range(NC)]


def mp_all(value):
    size = lax.axis_size("mp")
    return [value] + [lax.ppermute(value, "mp", ring(size, d)) for d in range(1, size)]


def swap(value):
    return lax.ppermute(value, "dp", CORE_SWAP)


def spread(value):
    return lax.all_to_all(value, "dp", 0, 0, axis_index_groups=PLANES)


def local(
    states, retrieval, pair_query, positions, targets,
    proj_weight, out_weight, up_weight, down_weight, vocab_embed,
):
    pairs, seq, width = states.shape
    masks = positions.shape[1]
    rows = pairs * masks
    cols = proj_weight.shape[2]
    heads = cols // HEAD
    hidden = up_weight.shape[1]
    half = width // 2
    vocab = vocab_embed.shape[0]
    index = lax.axis_index("dp").astype(jnp.int32)[None]
    core = index % NC
    base = (lax.axis_index("mp") * vocab).astype(jnp.int32)[None]
    flat = states.reshape(pairs * seq, width)

    xp, q, k, v, soft, ctx, part = call(
        k_attend,
        [((rows, width), BF), ((rows, cols), BF), ((pairs * seq, cols), BF), ((pairs * seq, cols), BF),
         ((pairs * heads * masks, seq), F32), ((rows, cols), BF), ((rows, width), BF)],
        (core, positions, flat, proj_weight, out_weight), 1, name="attend",
    )
    parts = mp_all(part)
    x_mine, x_other, fwd = call(
        k_split,
        [((pairs * seq, half), BF), ((pairs * seq, half), BF), ((rows, half + cols), BF)],
        (core, flat, xp, ctx), 1, name="split",
    )
    x_got, fwd_got = swap(x_other), swap(fwd)
    hat_one, scale_one, inner, part, own_f = call(
        k_feed,
        [((rows, width), F32), ((rows, 128), F32), ((rows, hidden), F32), ((rows, width), BF), ((rows, hidden + half), BF)],
        (core, xp, *parts, up_weight, down_weight), 1, name="feed",
    )
    parts = mp_all(part)
    got_f = swap(own_f)
    hat_two, scale_two, exps, stat = call(
        k_logits,
        [((rows, width), F32), ((rows, 128), F32), ((rows, vocab), BF), ((8, rows), F32)],
        (base, hat_one, *parts, targets, vocab_embed), 1, [pltpu.VMEM((rows, vocab), F32)], name="logits",
    )
    stats = mp_all(stat)
    sums, erow = call(
        k_vocab, [((rows, width), F32), ((rows, width), BF)], (base, exps, targets, vocab_embed), 1, name="vocab",
    )
    part, vals = call(
        k_join, [((rows, width), BF), ((NP * NC, 8, 128), F32)], (index, retrieval, *stats, sums, erow), 2, name="join",
    )
    parts = mp_all(part)
    vals = lax.all_to_all(vals, "dp", 0, 0)
    dpre_two, part, own_b, send_b, weight, score = call(
        functools.partial(k_back, pairs=pairs),
        [((rows, width), BF), ((rows, width), BF), ((rows, half + hidden), BF), ((rows, half + hidden), BF),
         ((8, 128), F32), ((8, 128), F32)],
        (core, index, vals, pair_query[None], *parts, hat_two, scale_two, inner, up_weight, down_weight), 2, name="back",
    )
    parts = mp_all(part)
    got_b = swap(send_b)
    early, = call(
        k_early, [((NP, ROW, 2 * hidden), BF)], (core, hat_one, own_f, got_f, own_b, got_b), 1, name="early",
    )
    early = spread(early)
    kv, own, send = call(
        k_attend_back,
        [((pairs * seq, 2 * cols), BF), ((rows, half + cols), BF), ((rows, half + cols), BF)],
        (core, weight, *parts, dpre_two, hat_one, scale_one, out_weight, q, k, v, soft), 1, name="attend_back",
    )
    kv_got, got = swap(kv), swap(send)
    late, = call(
        k_late, [((NP, ROW, 4 * cols), BF)], (core, x_mine, x_got, xp, ctx, fwd_got, kv, kv_got, own, got), 1, name="late",
    )
    late = spread(late)
    down_grad, up_grad = call(k_sum_early, [((hidden, ROW), F32), ((ROW, hidden), F32)], (early,), name="sum_early")
    out_grad, proj_grad = call(k_sum_late, [((cols, ROW), F32), ((3, ROW, cols), F32)], (late,), name="sum_late")
    return proj_grad, out_grad, up_grad, down_grad, score[0, :pairs]


def solution(mesh):
    return jax.shard_map(
        local,
        mesh=mesh,
        in_specs=(
            P("dp", None, None),
            P("dp"),
            P(),
            P("dp", None),
            P("dp", None),
            P(None, None, "mp"),
            P("mp", None),
            P(None, "mp"),
            P("mp", None),
            P("mp", None),
        ),
        out_specs=(P(None, "dp", "mp"), P("mp", "dp"), P("dp", "mp"), P("mp", "dp"), P("dp")),
        check_vma=False,
    )
```

```python
import functools

import jax
import jax.numpy as jnp
from jax import lax
from jax.experimental import pallas as pl
from jax.experimental.pallas import tpu as pltpu
from jax.sharding import PartitionSpec as P


HEAD = 64
NX, NZ, NC = 4, 4, 2
NP = NX * NZ
ROW = 32
BF = jnp.bfloat16
F32 = jnp.float32


def dot(left, right, dims):
    return lax.dot_general(left, right, (dims, ((), ())), preferred_element_type=F32)


def mm(left, right):
    return dot(left, right, ((1,), (0,)))


def mm_tn(left, right):
    return dot(left, right, ((0,), (0,)))


def mm_nt(left, right):
    return dot(left, right, ((1,), (1,)))


def iota(shape, dim):
    return lax.broadcasted_iota(jnp.int32, shape, dim)


def norm_parts(value):
    centre = jnp.mean(value, axis=-1, keepdims=True)
    centred = value - centre
    scale = lax.rsqrt(jnp.mean(centred * centred, axis=-1, keepdims=True) + 1e-05)
    return centred * scale, scale


def norm_back(hat, scale, cot):
    first = jnp.mean(cot, axis=-1, keepdims=True)
    second = jnp.mean(cot * hat, axis=-1, keepdims=True)
    return scale * (cot - first - hat * second)


def gelu_parts(value):
    root = 0.7978845608028654
    return jnp.tanh(root * (value + 0.044715 * value * value * value))


def gelu_slope(value):
    root = 0.7978845608028654
    bend = gelu_parts(value)
    return 0.5 * (1.0 + bend) + 0.5 * value * (1.0 - bend * bend) * root * (1.0 + 3.0 * 0.044715 * value * value)


def to_column(row):
    size = row.shape[1]
    eye = iota((size, size), 0) == iota((size, size), 1)
    return jnp.sum(jnp.where(eye, row, jnp.zeros_like(row)), axis=1, keepdims=True)


def to_row(column):
    size = column.shape[0]
    eye = iota((size, size), 0) == iota((size, size), 1)
    return jnp.sum(jnp.where(eye, column, jnp.zeros_like(column)), axis=0, keepdims=True)


def head_mask(rows, cols):
    return iota((rows, cols), 0) // (rows * HEAD // cols) == iota((rows, cols), 1) // HEAD


def stack_heads(block):
    masks, cols = block.shape
    heads = cols // HEAD
    tiled = jnp.concatenate([block] * heads, axis=0)
    return jnp.where(head_mask(heads * masks, cols), tiled.astype(F32), 0.0).astype(block.dtype)


def join_heads(block, masks):
    cols = block.shape[1]
    kept = jnp.where(head_mask(block.shape[0], cols), block, 0.0)
    return sum(kept[h * masks:(h + 1) * masks] for h in range(cols // HEAD))


def selector(width, core):
    half = width // 2
    col = iota((width, half), 1)
    return (iota((width, half), 0) == col // ROW * (2 * ROW) + core * ROW + col % ROW).astype(F32).astype(BF)


def own_core():
    return lax.rem(lax.axis_index("dp"), NC)


def total(parts):
    left, left_got, right, right_got = (r[...].astype(F32) for r in parts)
    return jnp.concatenate([left + left_got, right + right_got], axis=1)


def put_halves(value, left, right):
    half = left.shape[1]
    left[...] = value[:, :half].astype(BF)
    right[...] = value[:, half:].astype(BF)


def rows_of(weights, first, pairs, masks):
    return jnp.concatenate(
        [jnp.broadcast_to(weights[first + p:first + p + 1, 0:1], (masks, 1)) for p in range(pairs)], axis=0
    )


def k_attend(pos_hbm, x_hbm, wp_hbm, wo_hbm, o_x, o_xp, o_q, o_k, o_v, o_soft, o_ctx, o_left, o_right, pos, wp, wo, sem):
    pairs, masks = pos.shape
    seq = o_x.shape[0] // pairs
    fetch = {}

    def start(name, src, dst):
        fetch[name] = pltpu.make_async_copy(src, dst, sem.at[len(fetch)])
        fetch[name].start()

    start("pos", pos_hbm, pos)
    start("x0", x_hbm.at[0], o_x.at[pl.ds(0, seq)])
    for i in range(3):
        start(f"w{i}", wp_hbm.at[i], wp.at[i])
    for p in range(1, pairs):
        start(f"x{p}", x_hbm.at[p], o_x.at[pl.ds(p * seq, seq)])
    start("wo", wo_hbm, wo)
    fetch["pos"].wait()
    for p in range(pairs):
        rows, cols = pl.ds(p * masks, masks), pl.ds(p * seq, seq)
        fetch[f"x{p}"].wait()
        x_p = o_x[cols, :]
        place = (iota((seq, masks), 0) == pos[p:p + 1, :]).astype(F32).astype(BF)
        picked = mm_tn(place, x_p).astype(BF)
        o_xp[rows, :] = picked
        if p == 0:
            fetch["w0"].wait()
        query = mm(picked, wp[0]).astype(BF)
        if p == 0:
            fetch["w1"].wait()
        key = mm(x_p, wp[1]).astype(BF)
        if p == 0:
            fetch["w2"].wait()
        val = mm(x_p, wp[2]).astype(BF)
        o_q[rows, :] = query
        o_k[cols, :] = key
        o_v[cols, :] = val
        scores = mm_nt(stack_heads(query), key) * HEAD ** (-0.5)
        weights = jnp.exp(scores - jnp.max(scores, axis=-1, keepdims=True))
        soft = weights / jnp.sum(weights, axis=-1, keepdims=True)
        o_soft[pl.ds(p * soft.shape[0], soft.shape[0]), :] = soft
        o_ctx[rows, :] = join_heads(mm(soft.astype(BF), val), masks).astype(BF)
    fetch["wo"].wait()
    put_halves(mm(o_ctx[...], wo[...]), o_left, o_right)


def k_load(src, dst, sem):
    count = sem.shape[0]
    rows = dst.shape[0] // count
    copies = [
        pltpu.make_async_copy(src.at[pl.ds(i * rows, rows)], dst.at[pl.ds(i * rows, rows)], sem.at[i])
        for i in range(count)
    ]
    for c in copies:
        c.start()
    for c in copies:
        c.wait()


def k_split(x, xp, ctx, o_mine, o_other, o_keep, o_send):
    width = x.shape[1]
    mine, other = selector(width, own_core()), selector(width, 1 - own_core())
    o_mine[...] = mm(x[...], mine).astype(BF)
    o_other[...] = mm(x[...], other).astype(BF)
    o_keep[:, :width // 2] = mm(xp[...], mine).astype(BF)
    o_send[:, :width // 2] = mm(xp[...], other).astype(BF)
    o_keep[:, width // 2:] = ctx[...]
    o_send[:, width // 2:] = ctx[...]


def k_feed(xp, p0, p1, p2, p3, up, down, o_hat, o_scale, o_inner, o_left, o_right, o_send):
    pre_one = xp[...].astype(F32) + total((p0, p1, p2, p3))
    hat, scale = norm_parts(pre_one)
    o_hat[...] = hat
    o_scale[...] = jnp.broadcast_to(scale, o_scale.shape)
    first = hat.astype(BF)
    inner = mm(first, up[...])
    o_inner[...] = inner
    act = (0.5 * inner * (1.0 + gelu_parts(inner))).astype(BF)
    put_halves(mm(act, down[...]), o_left, o_right)
    hidden = inner.shape[1]
    o_send[:, :hidden] = act
    o_send[:, hidden:] = mm(first, selector(first.shape[1], 1 - own_core())).astype(BF)


CHUNK = 1024


def k_logits(hat, p0, p1, p2, p3, tgt, emb, o_hat, o_scale, o_exp, o_stat, logits):
    pre_two = hat[...].astype(BF).astype(F32) + total((p0, p1, p2, p3))
    hat_two, scale = norm_parts(pre_two)
    o_hat[...] = hat_two
    o_scale[...] = jnp.broadcast_to(scale, o_scale.shape)
    final = hat_two.astype(BF)
    rows = final.shape[0]
    target = jnp.concatenate([to_column(tgt[p:p + 1, :]) for p in range(tgt.shape[0])], axis=0) - lax.axis_index("mp") * emb.shape[0]
    top = jnp.full((rows, 1), -jnp.inf, F32)
    own = jnp.zeros((rows, 1), F32)
    steps = emb.shape[0] // CHUNK
    for j in range(steps):
        part = mm_nt(final, emb[j * CHUNK:(j + 1) * CHUNK, :])
        logits[:, j * CHUNK:(j + 1) * CHUNK] = part
        hot = iota((rows, CHUNK), 1) + j * CHUNK == target
        top = jnp.maximum(top, jnp.max(part, axis=1, keepdims=True))
        own += jnp.sum(jnp.where(hot, part, 0.0), axis=1, keepdims=True)
    rest = jnp.zeros((rows, 1), F32)
    for j in range(steps):
        hot = iota((rows, CHUNK), 1) + j * CHUNK == target
        value = jnp.where(hot, 0.0, jnp.exp(logits[:, j * CHUNK:(j + 1) * CHUNK] - top))
        o_exp[:, j * CHUNK:(j + 1) * CHUNK] = value.astype(BF)
        rest += jnp.sum(value, axis=1, keepdims=True)
    line = iota(o_stat.shape, 0)
    o_stat[...] = jnp.where(line == 0, to_row(top), jnp.where(line == 1, to_row(rest), jnp.where(line == 2, to_row(own), 0.0)))


def k_vocab(exps, tgt, emb, o_sum, o_row):
    rows = exps.shape[0]
    target = jnp.concatenate([to_column(tgt[p:p + 1, :]) for p in range(tgt.shape[0])], axis=0) - lax.axis_index("mp") * emb.shape[0]
    acc = jnp.zeros((2 * rows, emb.shape[1]), F32)
    for j in range(emb.shape[0] // CHUNK):
        hot = (iota((rows, CHUNK), 1) + j * CHUNK == target).astype(F32).astype(BF)
        left = jnp.concatenate([exps[:, j * CHUNK:(j + 1) * CHUNK], hot], axis=0)
        acc += mm(left, emb[j * CHUNK:(j + 1) * CHUNK, :])
    o_sum[...] = acc[:rows]
    o_row[...] = acc[rows:].astype(BF)


def k_join(retrieval, s0, s1, s2, s3, sums, erow, o_left, o_right, o_vals):
    stats = (s0, s1, s2, s3)
    top = s0[0:1, :]
    for s in stats[1:]:
        top = jnp.maximum(top, s[0:1, :])
    rest = sum(s[1:2, :] * jnp.exp(s[0:1, :] - top) for s in stats)
    goal = sum(s[2:3, :] for s in stats)
    denominator = rest + jnp.exp(goal - top)
    log_prob = goal - top - jnp.log(denominator)
    own = jnp.exp(s0[0:1, :] - top) / denominator
    put_halves(to_column(own) * sums[...] - to_column(rest / denominator) * erow[...].astype(F32), o_left, o_right)
    pairs = retrieval.shape[0]
    rows = log_prob.shape[1]
    masks = rows // pairs
    lane, line = iota((8, 128), 1), iota((8, 128), 0)
    vals = jnp.zeros((8, 128), F32)
    part_of = iota((1, rows), 1) // masks
    for p in range(pairs):
        doc = jnp.sum(jnp.where(part_of == p, log_prob, 0.0), axis=1, keepdims=True) / masks
        here = lane == lax.axis_index("dp") * pairs + p
        vals += jnp.where(here & (line == 0), retrieval[p], 0.0)
        vals += jnp.where(here & (line == 1), retrieval[p] + doc, 0.0)
    o_vals[...] = vals


def k_weight(vals, pq, o_w, o_score, pairs, masks):
    count = pq.shape[1]
    lane = iota((1, count), 1)
    priors, posts = vals[0:1, :count], vals[1:2, :count]
    line = iota((8, 128), 0)
    weights = jnp.zeros((8, 128), F32)
    index = lax.axis_index("dp")
    for who, owner in enumerate((index, index + 1 - 2 * own_core())):
        for p in range(pairs):
            here = lane == owner * pairs + p
            query = jnp.sum(jnp.where(here, pq[...], 0), axis=1, keepdims=True)
            same = pq[...] == query

            def share(values):
                top = jnp.max(jnp.where(same, values, -1e30), axis=1, keepdims=True)
                terms = jnp.where(same, jnp.exp(jnp.where(same, values - top, 0.0)), 0.0)
                own = jnp.sum(jnp.where(here, values, 0.0), axis=1, keepdims=True)
                return jnp.exp(own - (top + jnp.log(jnp.sum(terms, axis=1, keepdims=True))))

            posterior = share(posts)
            weights += jnp.where(line == who * pairs + p, posterior / masks, 0.0)
            if who == 0:
                o_score[p] = jnp.sum(share(priors) - posterior)
    o_w[...] = weights


def k_back(p0, p1, p2, p3, hat, scale, inner, up, down, o_dpre, o_left, o_right, o_half, o_send):
    dpre = norm_back(hat[...], scale[:, 0:1], total((p0, p1, p2, p3))).astype(BF)
    o_dpre[...] = dpre
    dinner = (gelu_slope(inner[...]) * mm_nt(dpre, down[...])).astype(BF)
    put_halves(mm_nt(dinner, up[...]), o_left, o_right)
    width = dpre.shape[1]
    o_half[:, :width // 2] = mm(dpre, selector(width, own_core())).astype(BF)
    o_half[:, width // 2:] = dinner
    o_send[:, :width // 2] = mm(dpre, selector(width, 1 - own_core())).astype(BF)
    o_send[:, width // 2:] = dinner


def k_early(w, hat, own_f, got_f, own_b, got_b, o_own, o_up_x, o_down_x, o_far_up, o_far_down, held, pairs):
    rows, width = hat.shape
    half = width // 2
    hidden = own_f.shape[1] - half
    masks = rows // pairs
    own = (own_b[...].astype(F32) * rows_of(w, 0, pairs, masks)).astype(BF)
    got = (got_b[...].astype(F32) * rows_of(w, pairs, pairs, masks)).astype(BF)
    both = jnp.concatenate([own, got], axis=0)
    first = mm(hat[...].astype(BF), selector(width, own_core())).astype(BF)
    left = jnp.concatenate([first, got_f[:, hidden:]], axis=0)
    right = jnp.concatenate([own_f[:, :hidden], got_f[:, :hidden]], axis=0)
    shape = held.shape[:3] + (hidden,)
    held[:, :, :, :hidden] = mm_tn(both[:, :half], right).astype(BF).reshape(shape)
    held[:, :, :, hidden:] = mm_tn(left, both[:, half:]).astype(BF).reshape(shape)
    own_x = lax.div(lax.axis_index("dp"), NZ * NC)
    far = lax.rem(own_x + 2, NX)
    o_own[...] = held[own_x]
    o_up_x[...] = held[lax.rem(own_x + 1, NX)]
    o_down_x[...] = held[lax.rem(own_x + 3, NX)]
    o_far_up[...] = held[far, :NZ // 2]
    o_far_down[...] = held[far, NZ // 2:]


def k_relay(up, down, got_up, got_down, o_up, o_down):
    mid = got_up.shape[0]
    o_up[:mid] = (up[:mid].astype(F32) + got_up[...].astype(F32)).astype(BF)
    o_up[mid:] = up[mid:]
    o_down[:mid] = down[:mid]
    o_down[mid:] = (down[mid:].astype(F32) + got_down[...].astype(F32)).astype(BF)


def k_planes(own, got_up, got_down, o_own, o_1, o_2, o_3, held):
    held[...] = own[...].astype(F32) + got_up[...].astype(F32) + got_down[...].astype(F32)
    own_z = lax.rem(lax.div(lax.axis_index("dp"), NC), NZ)
    o_own[...] = held[own_z]
    for d, out in enumerate((o_1, o_2, o_3)):
        out[...] = held[lax.rem(own_z + d + 1, NZ)].astype(BF)


def k_attend_back(w, p0, p1, p2, p3, dpre_two, hat, scale, wo, q, k, v, soft, o_kv, o_mine, o_send):
    rows, width = hat.shape
    cols = q.shape[1]
    pairs = k.shape[0] // soft.shape[1]
    masks = rows // pairs
    seq = soft.shape[1]
    dfirst = dpre_two[...].astype(F32) + total((p0, p1, p2, p3))
    dpre = norm_back(hat[...], scale[:, 0:1], dfirst).astype(BF)
    dctx = mm_nt(dpre, wo[...]).astype(BF)
    weight = rows_of(w, 0, pairs, masks)
    scaled = (dpre.astype(F32) * weight).astype(BF)
    half = width // 2
    o_mine[:, :half] = mm(scaled, selector(width, own_core())).astype(BF)
    o_send[:, :half] = mm(scaled, selector(width, 1 - own_core())).astype(BF)
    size = soft.shape[0] // pairs
    for p in range(pairs):
        own = w[p:p + 1, 0:1]
        lines = pl.ds(p * masks, masks)
        stacked = stack_heads(dctx[p * masks:(p + 1) * masks])
        prob = soft[p * size:(p + 1) * size, :]
        o_kv[pl.ds(p * seq, seq), cols:] = (mm_tn(prob.astype(BF), stacked) * own).astype(BF)
        dprob = mm_nt(stacked, v[p * seq:(p + 1) * seq, :]).astype(BF).astype(F32)
        dscore = prob * (dprob - jnp.sum(dprob * prob, axis=-1, keepdims=True))
        dscore = (dscore * HEAD ** (-0.5)).astype(BF)
        dquery = (join_heads(mm(dscore, k[p * seq:(p + 1) * seq, :]), masks) * own).astype(BF)
        o_mine[lines, half:] = dquery
        o_send[lines, half:] = dquery
        o_kv[pl.ds(p * seq, seq), :cols] = (mm_tn(dscore, stack_heads(q[lines, :])) * own).astype(BF)


def k_late(keep, fwd, kv, kv_got, own, got, x_mine, x_got, out_hbm, out, sem):
    half = x_mine.shape[1]
    cols = keep.shape[1] - half
    count = out.shape[0]
    per = half // count
    heads = jnp.concatenate([keep[...], fwd[...]], axis=0)
    cots = jnp.concatenate([own[...], got[...]], axis=0)
    d_out = mm_tn(cots[:, :half], heads[:, half:]).astype(BF)
    d_q = mm_tn(heads[:, :half], cots[:, half:]).astype(BF)
    d_kv = (mm_tn(x_mine[...], kv[...]) + mm_tn(x_got[...], kv_got[...])).astype(BF)
    copies = []
    for i in range(count):
        lines = slice(i * per, (i + 1) * per)
        out[i, :, :cols] = d_out[lines]
        out[i, :, cols:2 * cols] = d_q[lines]
        out[i, :, 2 * cols:] = d_kv[lines]
        copies.append(pltpu.make_async_copy(out.at[i], out_hbm.at[i], sem.at[i]))
        copies[-1].start()
    for c in copies:
        c.wait()


def k_sum(late, own, got_1, got_2, got_3, o_down, o_up, o_out, o_proj):
    hidden, cols = o_up.shape[1], o_out.shape[1]
    value = own[...] + got_1[...].astype(F32) + got_2[...].astype(F32) + got_3[...].astype(F32)
    o_down[...] = value[:, :hidden]
    o_up[...] = value[:, hidden:]
    value = jnp.sum(late[...].astype(F32), axis=0)
    o_out[...] = value[:, :cols]
    for i in range(o_proj.shape[0]):
        o_proj[i] = value[:, (i + 1) * cols:(i + 2) * cols]


def call(body, outs, args, ins="", puts="", scratch=(), mib=12, lazy=0):
    ins, puts = ins.ljust(len(args), "v"), puts.ljust(len(outs), "v")
    specs = {
        "v": pl.BlockSpec(memory_space=pltpu.VMEM),
        "a": pl.BlockSpec(memory_space=pltpu.VMEM),
        "s": pl.BlockSpec(memory_space=pltpu.SMEM),
        "h": pl.BlockSpec(memory_space=pltpu.HBM),
        "d": pl.BlockSpec(memory_space=pltpu.HBM),
    }
    made = {"v": pltpu.VMEM, "a": jax.ShapeDtypeStruct, "s": pltpu.SMEM, "h": pltpu.HBM, "d": pltpu.HBM}
    held_in = [i for i, k in enumerate(ins) if k == "h"]
    held_out = [i for i, k in enumerate(puts) if k == "h"]
    moved = sum(a.size * a.dtype.itemsize for a in args)
    copies = [pltpu.VMEM(args[i].shape, args[i].dtype) for i in held_in]
    copies += [pltpu.VMEM(*outs[i]) for i in held_out]
    sems = [pltpu.SemaphoreType.DMA((len(copies),))] if copies else []

    def kernel(*refs):
        refs = list(refs)
        bodies = len(args) + len(outs)
        bufs, rest = refs[bodies:bodies + len(copies)], refs[bodies + len(copies):]
        fetch, store = [], []
        if copies:
            sem, rest = rest[0], rest[1:]
            for n, i in enumerate(held_in):
                fetch.append(pltpu.make_async_copy(refs[i], bufs[n], sem.at[n]))
                refs[i] = bufs[n]
            for n, i in enumerate(held_out):
                n += len(held_in)
                store.append(pltpu.make_async_copy(bufs[n], refs[len(args) + i], sem.at[n]))
                refs[len(args) + i] = bufs[n]
        for c in fetch:
            c.start()
        for c in fetch[:len(fetch) - lazy]:
            c.wait()

        def ready():
            for c in fetch[len(fetch) - lazy:]:
                c.wait()

        body(*refs[:bodies], *rest, **({"ready": ready} if lazy else {}))
        for c in store:
            c.start()
        for c in store:
            c.wait()

    args = [pltpu.with_memory_space_constraint(a, pltpu.HBM) if k in "hd" else a for a, k in zip(args, ins)]
    return pl.pallas_call(
        kernel,
        out_shape=[made[k](s, d) for (s, d), k in zip(outs, puts)],
        in_specs=[specs[k] for k in ins],
        out_specs=[specs[k] for k in puts],
        scratch_shapes=copies + sems + list(scratch),
        compiler_params=pltpu.CompilerParams(vmem_limit_bytes=mib << 20),
        cost_estimate=pl.CostEstimate(flops=0, bytes_accessed=moved, transcendentals=0),
    )(*args)


def ring(size, shift):
    return [(i, (i + shift) % size) for i in range(size)]


def dp_index(x, z, c):
    return (x * NZ + z) * NC + c


CORE_SWAP = [
    (dp_index(x, z, c), dp_index(x, z, 1 - c)) for x in range(NX) for z in range(NZ) for c in range(NC)
]
PLANES = [[dp_index(x, z, c) for x in range(NX) for z in range(NZ)] for c in range(NC)]


def x_ring(shift):
    return [
        (dp_index(x, z, c), dp_index((x + shift) % NX, z, c))
        for x in range(NX) for z in range(NZ) for c in range(NC)
    ]


def z_ring(shift):
    return [
        (dp_index(x, z, c), dp_index(x, (z + shift) % NZ, c))
        for x in range(NX) for z in range(NZ) for c in range(NC)
    ]


NEAR = [(i, i ^ 1) for i in range(4)]
FAR = [(i, 3 - i) for i in range(4)]


def mp_all(value):
    size = lax.axis_size("mp")
    return [value] + [lax.ppermute(value, "mp", ring(size, d)) for d in range(1, size)]


def k_half_add(value, got, out):
    out[...] = (value[...].astype(F32) + got[...].astype(F32)).astype(BF)


def k_add(*refs):
    refs[-1][...] = sum(r[...] for r in refs[:-1])


def mp_halves(left, right):
    left_got, right_got = lax.ppermute(left, "mp", NEAR), lax.ppermute(right, "mp", FAR)
    left, = call(k_half_add, [(left.shape, BF)], (left, left_got), mib=2)
    right, = call(k_half_add, [(right.shape, BF)], (right, right_got), mib=2)
    return left, lax.ppermute(left, "mp", FAR), right, lax.ppermute(right, "mp", NEAR)


def swap(value):
    return lax.ppermute(value, "dp", CORE_SWAP)


def spread(value):
    return lax.all_to_all(value, "dp", 0, 0, axis_index_groups=PLANES)


def add(*values):
    return call(k_add, [(values[0].shape, values[0].dtype)], values, mib=2)[0]


def gather_sum(vals):
    vals = add(vals, lax.ppermute(vals, "dp", CORE_SWAP))
    vals = add(vals, *[lax.ppermute(vals, "dp", z_ring(d)) for d in range(1, NZ)])
    return add(vals, *[lax.ppermute(vals, "dp", x_ring(d)) for d in range(1, NX)])


def local(
    states, retrieval, pair_query, positions, targets,
    proj_weight, out_weight, up_weight, down_weight, vocab_embed,
):
    pairs, seq, width = states.shape
    masks = positions.shape[1]
    rows = pairs * masks
    cols = proj_weight.shape[2]
    heads = cols // HEAD
    hidden = up_weight.shape[1]
    half = width // 2
    vocab = vocab_embed.shape[0]
    part2 = [((rows, half), BF)] * 2
    dma = pltpu.SemaphoreType.DMA

    flat, xp, q, k, v, soft, ctx, *part = call(
        k_attend,
        [((pairs * seq, width), BF), ((rows, width), BF), ((rows, cols), BF), ((pairs * seq, cols), BF),
         ((pairs * seq, cols), BF), ((pairs * heads * masks, seq), F32), ((rows, cols), BF), *part2],
        (positions, states, proj_weight, out_weight), "dddd", "",
        [pltpu.VMEM(positions.shape, jnp.int32), pltpu.VMEM(proj_weight.shape, BF), pltpu.VMEM(out_weight.shape, BF), dma((5 + pairs,))],
    )
    parts = mp_halves(*part)
    x_mine, x_other, keep, fwd = call(
        k_split,
        [((pairs * seq, half), BF), ((pairs * seq, half), BF), ((rows, half + cols), BF), ((rows, half + cols), BF)],
        (flat, xp, ctx),
    )
    x_got, fwd_got = swap(x_other), swap(fwd)
    hat_one, scale_one, inner, left, right, own_f = call(
        k_feed,
        [((rows, width), F32), ((rows, 128), F32), ((rows, hidden), F32), *part2,
         ((rows, hidden + half), BF)],
        (xp, *parts, up_weight, down_weight),
    )
    parts = mp_halves(left, right)
    emb, = call(k_load, [(vocab_embed.shape, BF)], (vocab_embed,), "d", scratch=[dma((8,))])
    got_f = swap(own_f)
    hat_two, scale_two, exps, stat = call(
        k_logits,
        [((rows, width), F32), ((rows, 128), F32), ((rows, vocab), BF), ((8, rows), F32)],
        (hat_one, *parts, targets, emb), scratch=[pltpu.VMEM((rows, vocab), F32)],
    )
    stats = mp_all(stat)
    sums, erow = call(k_vocab, [((rows, width), F32), ((rows, width), BF)], (exps, targets, emb))
    left, right, vals = call(k_join, [*part2, ((8, 128), F32)], (retrieval, *stats, sums, erow), "s")
    parts = mp_halves(left, right)
    vals = gather_sum(vals)
    weight, score = call(
        functools.partial(k_weight, pairs=pairs, masks=masks), [((8, 128), F32), ((pairs,), F32)],
        (vals, pair_query[None]), puts="vs",
    )
    dpre_two, left, right, own_b, send_b = call(
        k_back,
        [((rows, width), BF), *part2, ((rows, half + hidden), BF), ((rows, half + hidden), BF)],
        (*parts, hat_two, scale_two, inner, up_weight, down_weight),
    )
    parts = mp_halves(left, right)
    got_b = swap(send_b)
    slab, part_slab, row_slab = (NZ, ROW, 2 * hidden), (NZ // 2, ROW, 2 * hidden), (ROW, 2 * hidden)
    own_x, up_x, down_x, far_up, far_down = call(
        functools.partial(k_early, pairs=pairs),
        [(slab, BF), (slab, BF), (slab, BF), (part_slab, BF), (part_slab, BF)],
        (weight, hat_one, own_f, got_f, own_b, got_b), scratch=[pltpu.VMEM((NX,) + slab, BF)], mib=16,
    )
    far_up, far_down = lax.ppermute(far_up, "dp", x_ring(1)), lax.ppermute(far_down, "dp", x_ring(-1))
    up_x, down_x = call(k_relay, [(slab, BF), (slab, BF)], (up_x, down_x, far_up, far_down), mib=4)
    up_x, down_x = lax.ppermute(up_x, "dp", x_ring(1)), lax.ppermute(down_x, "dp", x_ring(-1))
    kv, own, send = call(
        k_attend_back,
        [((pairs * seq, 2 * cols), BF), ((rows, half + cols), BF), ((rows, half + cols), BF)],
        (weight, *parts, dpre_two, hat_one, scale_one, out_weight, q, k, v, soft),
    )
    kv_got, got = swap(kv), swap(send)
    shape = (NP, half // NP, 4 * cols)
    late, = call(
        k_late, [(shape, BF)], (keep, fwd_got, kv, kv_got, own, got, x_mine, x_got), puts="d",
        scratch=[pltpu.VMEM(shape, BF), dma((NP,))],
    )
    late = spread(late)
    own_z, *planes = call(
        k_planes, [(row_slab, F32), (row_slab, BF), (row_slab, BF), (row_slab, BF)], (own_x, up_x, down_x),
        scratch=[pltpu.VMEM(slab, F32)], mib=8,
    )
    planes = [lax.ppermute(v, "dp", z_ring(d + 1)) for d, v in enumerate(planes)]
    down_grad, up_grad, out_grad, proj_grad = call(
        k_sum,
        [((ROW, hidden), F32), ((ROW, hidden), F32), ((ROW, cols), F32), ((3, ROW, cols), F32)],
        (late, own_z, *planes), puts="aaaa",
    )
    return proj_grad, out_grad.T, up_grad, down_grad.T, score


def solution(mesh):
    return jax.shard_map(
        local,
        mesh=mesh,
        in_specs=(
            P("dp", None, None),
            P("dp"),
            P(),
            P("dp", None),
            P("dp", None),
            P(None, None, "mp"),
            P("mp", None),
            P(None, "mp"),
            P("mp", None),
            P("mp", None),
        ),
        out_specs=(P(None, "dp", "mp"), P("mp", "dp"), P("dp", "mp"), P("mp", "dp"), P("dp")),
        check_vma=False,
    )
```
